32 devices in a mesh: chan: 8 (over z, y), off: 4 (over x, core).
Axes of the slice: x: 2, y: 2, z: 4, core: 2. Of those that a mesh axis runs over, the one named last changes fastest.
Arguments:
- traces: bfloat16 [512, 4096], P('chan'), may hold values from -6 to 6
- band_gain: float32 [2048], P('off'), may hold values from 0.5 to 2
- pair_list: int32 [2048, 2], P('chan'), may hold values from 0 to 511, as said below
- pair_count: int32 [32], P(('chan', 'off')), may hold values from 16 to 64, as said below
Outputs:
- gathers: float32 [2048, 1024], P(('chan', 'off'))
The draws below stay inside these ranges and needn't reach their ends.
Inputs may be any that keep to these rules, and one draw needn't show every extreme that they name: `pair_list`: row r names first a channel of block r // 256 (channels c * 64 to c * 64 + 63 form block c), then a channel whose block lies at most 2 blocks away from it around the loop of blocks, either way. Slots that are not live hold pairs of the same kind. `pair_count`: in every channel block one owner has all 64 slots live.
All inputs are finite; a program needn't handle non-finite values.
Results may differ from the reference program's by a relative error of at most 0.0064.
Values may be sent and summed in bfloat16 or wider, within the bound.
A program may use at most 64 MiB of HBM per device.

```python
import math
import jax
import jax.numpy as jnp
from jax import lax

NSAMP = 4096
NLAG = 1024
BAND = 64
CH_DEV = 64
CAP = 64
NFREQ = 2048
REACH = 2
CHANNELS = 512
PAIRS = 256
N_OFF = 4


def draw_pair_list(key, part):
    block_total = CHANNELS // CH_DEV
    row_count = block_total * PAIRS
    key_first, key_offset, key_second = jax.random.split(jax.random.fold_in(key, 11), 3)
    block_ids = jnp.arange(row_count, dtype=jnp.int32) // PAIRS
    first_chan = block_ids * CH_DEV + jax.random.randint(key_first, (row_count,), 0, CH_DEV)
    offsets = jax.random.randint(key_offset, (row_count,), -REACH, REACH + 1)
    partner_block = jnp.mod(block_ids + offsets, block_total)
    second_chan = partner_block * CH_DEV + jax.random.randint(key_second, (row_count,), 0, CH_DEV)
    return jnp.stack([first_chan, second_chan], axis=1).astype(jnp.int32)


def draw_pair_count(key, part):
    block_total = CHANNELS // CH_DEV
    owners = PAIRS // CAP
    key_counts, key_busiest = jax.random.split(jax.random.fold_in(key, 23), 2)
    counts = jax.random.randint(key_counts, (block_total, owners), max(1, CAP // 4), CAP // 2 + 1)
    busiest = jax.random.randint(key_busiest, (block_total, 1), 0, owners)
    owner_ids = jnp.arange(owners, dtype=jnp.int32)[None, :]
    counts = jnp.where(owner_ids == busiest, CAP, counts)
    return counts.reshape(-1).astype(jnp.int32)


def shard_levels(own_key, extent, pieces, low, largest):
    level = 1.0
    for dim, shards_of in pieces:
        draws = jax.random.uniform(jax.random.fold_in(jax.random.fold_in(own_key, 6), dim), (shards_of,), jnp.float32, low / len(pieces), largest / len(pieces))
        level = level * jnp.repeat(jnp.exp(draws), extent[dim] // shards_of).reshape((-1,) + (1,) * (len(extent) - 1 - dim))
    return level


def bell_draw(rng, shape, scale, reach, pieces=(), kind=jnp.bfloat16):
    level = shard_levels(rng, shape, pieces, -0.22, 0.18) if pieces else 1.0
    drawn = jax.random.normal(rng, shape, jnp.float32) * scale * level
    return jnp.minimum(jnp.maximum(drawn, -reach), reach).astype(kind)


def setup_inputs(seed: int = 0) -> dict:
    seeds = jax.random.split(jax.random.key(seed), 5)
    traces = bell_draw(seeds[0], (CHANNELS, NSAMP), 1.0, 6.0, ((0, 8),))
    band_gain = jnp.clip(jnp.exp(math.log(2.0) - 1.3862944 * jax.random.uniform(seeds[1], (NFREQ,), jnp.float32) ** shard_levels(seeds[1], (NFREQ,), ((0, 4),), -0.2, 0.2)), 0.5, 2.0)
    pair_list = draw_pair_list(jax.random.fold_in(seeds[4], 71), 0)
    pair_count = draw_pair_count(jax.random.fold_in(seeds[4], 71), 0)
    return dict(traces=traces, band_gain=band_gain, pair_list=pair_list, pair_count=pair_count)


def forward_basis(time_lo, time_count, bin_lo, bin_count, sample_count):
    sample_ids = (time_lo + jnp.arange(time_count, dtype=jnp.int32))[:, None]
    bin_ids = (bin_lo + jnp.arange(bin_count, dtype=jnp.int32))[None, :]
    angles = jnp.mod(sample_ids * bin_ids, sample_count).astype(jnp.float32) * (2.0 * math.pi / sample_count)
    return jnp.concatenate([jnp.cos(angles), -jnp.sin(angles)], axis=1).astype(jnp.bfloat16)

def inverse_basis(bin_lo, bin_count, sample_count, lag_count):
    bin_ids = (bin_lo + jnp.arange(bin_count, dtype=jnp.int32))[:, None]
    lag_ids = jnp.arange(lag_count, dtype=jnp.int32)[None, :] - lag_count // 2
    angles = jnp.mod(bin_ids * lag_ids, sample_count).astype(jnp.float32) * (2.0 * math.pi / sample_count)
    return jnp.concatenate([jnp.cos(angles), -jnp.sin(angles)], axis=0).astype(jnp.bfloat16)

def whiten(raw_spectra, gain):
    bin_count = gain.shape[0]
    row_count = raw_spectra.shape[0]
    real_part = raw_spectra[:, :bin_count]
    imag_part = raw_spectra[:, bin_count:]
    band_power = (real_part * real_part + imag_part * imag_part).reshape(row_count, bin_count // BAND, BAND)
    band_scale = lax.rsqrt(lax.optimization_barrier(jnp.mean(band_power, axis=2)) + 1e-06)
    band_scale = jnp.repeat(band_scale, BAND, axis=1) * gain[None, :]
    return jnp.concatenate([real_part * band_scale, imag_part * band_scale], axis=1).astype(jnp.bfloat16)

def cross_spectra(left_rows, right_rows):
    half = left_rows.shape[1] // 2
    left_rows = left_rows.astype(jnp.float32)
    right_rows = right_rows.astype(jnp.float32)
    left_real, left_imag = (left_rows[:, :half], left_rows[:, half:])
    right_real, right_imag = (right_rows[:, :half], right_rows[:, half:])
    real_part = left_real * right_real + left_imag * right_imag
    imag_part = left_real * right_imag - left_imag * right_real
    return jnp.concatenate([real_part, imag_part], axis=1).astype(jnp.bfloat16)

def reference(traces, band_gain, pair_list, pair_count):
    basis = forward_basis(0, NSAMP, 0, NFREQ, NSAMP)
    spectra = jnp.dot(traces, basis, preferred_element_type=jnp.float32)
    whitened = whiten(spectra, band_gain)
    cross = cross_spectra(whitened[pair_list[:, 0]], whitened[pair_list[:, 1]])
    inverse = inverse_basis(0, NFREQ, NSAMP, NLAG)
    lagsum = jnp.dot(cross, inverse, preferred_element_type=jnp.float32)
    slot_ids = jnp.arange(pair_list.shape[0], dtype=jnp.int32)
    block_ids = slot_ids // PAIRS
    within = slot_ids % PAIRS
    owner_ids = within // CAP
    live_slots = within % CAP < pair_count[block_ids * N_OFF + owner_ids]
    return jnp.where(live_slots[:, None], lagsum * (1.0 / math.sqrt(NFREQ)), 0.0)
```

```python
import functools
import math

import jax
import jax.numpy as jnp
import numpy as np
from jax import lax
from jax.experimental import pallas as pl
from jax.experimental.pallas import tpu as pltpu
from jax.sharding import PartitionSpec as P

NLAG = 1024
BAND = 64
RADIX = 4
LANES = 128
STEP = 64
MESH = pl.DeviceIdType.MESH


def angle_table(rows, cols, period):
    turns = np.mod(np.outer(rows, cols), period).astype(np.float64) * (2.0 * math.pi / period)
    return np.cos(turns), np.sin(turns)


def kernel(
    sizes,
    traces_ref, gain_ref, pairs_ref, limit_ref,
    inner_cos_ref, inner_sin_ref, outer_cos_ref, outer_sin_ref,
    coarse_cos_ref, coarse_sin_ref, fine_cos_ref, fine_sin_ref,
    out_ref,
    table, inverse, part_send, part_recv, sum_send, sum_recv,
    chan_send_sem, chan_recv_sem, pair_send_sem, pair_recv_sem, off_send_sem, off_recv_sem,
):
    chan_total, owners, reach = sizes
    rows, sample_count = traces_ref.shape
    bins = gain_ref.shape[1]
    lags = out_ref.shape[1]
    group = out_ref.shape[0]
    half = owners // 2
    me_chan = lax.axis_index("chan")
    me_off = lax.axis_index("off")
    bin_lo = me_off * bins
    parity = lax.rem(me_off, 2)
    my_half = lax.div(me_off, 2)
    partner = me_off + 1 - 2 * parity

    def chan_peer(shift):
        return lax.rem(me_chan + shift + chan_total, chan_total)

    def off_peer(step):
        return 2 * lax.rem(my_half + step, half) + parity

    shifts = [s for d in range(1, reach + 1) for s in (d, -d)]
    barrier = pltpu.get_barrier_semaphore()
    for shift in shifts:
        pl.semaphore_signal(barrier, inc=1, device_id=(chan_peer(shift), me_off), device_id_type=MESH)
    pl.semaphore_signal(barrier, inc=1, device_id=(me_chan, partner), device_id_type=MESH)
    for step in range(1, half):
        pl.semaphore_signal(barrier, inc=1, device_id=(me_chan, off_peer(step)), device_id_type=MESH)

    inner = sample_count // RADIX
    chunk = RADIX * LANES
    chunks = sample_count // chunk
    odd_half = lax.rem(lax.div(bin_lo, inner // 2), 2)
    src = lax.broadcasted_iota(jnp.int32, (chunk, chunk), 0)
    dst = lax.broadcasted_iota(jnp.int32, (chunk, chunk), 1)
    lane = lax.rem(dst, LANES)
    wanted = RADIX * lane + lax.div(dst, LANES)
    flip = 1.0 - 2.0 * (lax.rem(lane, 2) * odd_half).astype(jnp.float32)
    spread = jnp.where(src == wanted, flip, 0.0).astype(jnp.bfloat16)
    stacked = jnp.concatenate([traces_ref[:, c * chunk:(c + 1) * chunk] for c in range(chunks)], axis=0)
    split = jnp.dot(stacked, spread, preferred_element_type=jnp.float32).astype(jnp.bfloat16)
    by_residue = jnp.concatenate(
        [
            jnp.concatenate(
                [split[c * rows:(c + 1) * rows, r * LANES:(r + 1) * LANES] for c in range(chunks)], axis=1
            )
            for r in range(RADIX)
        ],
        axis=0,
    )
    col_lo = pl.multiple_of(lax.rem(bin_lo, inner // 2), LANES)
    in_re = jnp.dot(by_residue, inner_cos_ref[:, pl.ds(col_lo, bins)], preferred_element_type=jnp.float32)
    in_im = jnp.dot(by_residue, inner_sin_ref[:, pl.ds(col_lo, bins)], preferred_element_type=jnp.float32)
    tw_lo = pl.multiple_of(bin_lo, LANES)
    real_part = in_re[:rows]
    imag_part = in_im[:rows]
    for r in range(1, RADIX):
        tc = outer_cos_ref[r:r + 1, pl.ds(tw_lo, bins)]
        ts = outer_sin_ref[r:r + 1, pl.ds(tw_lo, bins)]
        a = in_re[r * rows:(r + 1) * rows]
        b = in_im[r * rows:(r + 1) * rows]
        real_part += a * tc - b * ts
        imag_part += a * ts + b * tc

    power = real_part * real_part + imag_part * imag_part
    high = power.astype(jnp.bfloat16)
    low = (power - high.astype(jnp.float32)).astype(jnp.bfloat16)
    band_a = lax.div(lax.broadcasted_iota(jnp.int32, (bins, bins), 0), BAND)
    band_b = lax.div(lax.broadcasted_iota(jnp.int32, (bins, bins), 1), BAND)
    mean_of = jnp.where(band_a == band_b, 1.0 / BAND, 0.0).astype(jnp.bfloat16)
    mean = jnp.dot(high, mean_of, preferred_element_type=jnp.float32) + jnp.dot(
        low, mean_of, preferred_element_type=jnp.float32
    )
    scale = lax.rsqrt(mean + 1e-06) * gain_ref[...]
    own = table.at[reach]
    own[:, :bins] = (real_part * scale).astype(jnp.bfloat16)
    own[:, bins:] = (imag_part * scale).astype(jnp.bfloat16)

    pl.semaphore_wait(barrier, len(shifts) + half)

    moves = []
    for i, shift in enumerate(shifts):
        moves.append(
            pltpu.make_async_remote_copy(
                src_ref=own,
                dst_ref=table.at[reach - shift],
                send_sem=chan_send_sem.at[i],
                recv_sem=chan_recv_sem.at[i],
                device_id=(chan_peer(shift), me_off),
                device_id_type=MESH,
            )
        )
    for move in reversed(moves):
        move.start()

    row_lo = lax.div(bin_lo, STEP)

    def fill(a, carry):
        cc = coarse_cos_ref[pl.ds(row_lo + a, 1), :]
        cs = coarse_sin_ref[pl.ds(row_lo + a, 1), :]
        fc = fine_cos_ref[...]
        fs = fine_sin_ref[...]
        at = pl.multiple_of(a * STEP, STEP)
        inverse[pl.ds(at, STEP), :] = (cc * fc - cs * fs).astype(jnp.bfloat16)
        inverse[pl.ds(bins + at, STEP), :] = (-(cs * fc + cc * fs)).astype(jnp.bfloat16)
        return carry

    lax.fori_loop(0, bins // STEP, fill, 0)

    for move in moves:
        move.wait_recv()

    span = (2 * reach + 1) * rows
    chan_a = me_chan * rows + lax.broadcasted_iota(jnp.int32, (1, rows), 1)
    chan_b = (me_chan - reach) * rows + lax.broadcasted_iota(jnp.int32, (1, span), 1)
    chan_b = jnp.where(chan_b < 0, chan_b + chan_total * rows, chan_b)
    chan_b = jnp.where(chan_b >= chan_total * rows, chan_b - chan_total * rows, chan_b)

    def lag_rows(par):
        pairs = jnp.concatenate(
            [pairs_ref[pl.ds(pl.multiple_of((2 * h + par) * group, group), group), :] for h in range(half)], axis=0
        )
        pick_a = jnp.where(pairs[:, 0:1] == chan_a, 1.0, 0.0).astype(jnp.bfloat16)
        pick_b = jnp.where(pairs[:, 1:2] == chan_b, 1.0, 0.0).astype(jnp.bfloat16)
        left = jnp.dot(pick_a, own[...], preferred_element_type=jnp.float32)
        right = jnp.dot(
            pick_b, table[...].reshape(span, 2 * bins), preferred_element_type=jnp.float32
        )
        la, lb = left[:, :bins], left[:, bins:]
        ra, rb = right[:, :bins], right[:, bins:]
        cross = jnp.concatenate([la * ra + lb * rb, la * rb - lb * ra], axis=1).astype(jnp.bfloat16)
        return jnp.dot(cross, inverse[...], preferred_element_type=jnp.float32)

    part_send[...] = lag_rows(1 - parity).astype(part_send.dtype)
    swap = pltpu.make_async_remote_copy(
        src_ref=part_send,
        dst_ref=part_recv,
        send_sem=pair_send_sem,
        recv_sem=pair_recv_sem,
        device_id=(me_chan, partner),
        device_id_type=MESH,
    )
    swap.start()
    mine = lag_rows(parity)
    swap.wait_recv()
    mine = mine + part_recv[...].astype(jnp.float32)
    for h in range(half):
        sum_send[h] = mine[h * group:(h + 1) * group]
    narrow = sum_recv.dtype
    sends = []
    for step in range(1, half):
        slot = lax.rem(my_half + step, half)
        part_send_slot = sum_send.at[slot]
        sends.append(part_send_slot)
    out_ref[...] = sum_send[my_half]
    moves_off = []
    stage = part_recv
    for step in range(1, half):
        slot = lax.rem(my_half + step, half)
        stage[pl.ds((step - 1) * group, group), :] = sum_send[slot].astype(narrow)
        moves_off.append(
            pltpu.make_async_remote_copy(
                src_ref=stage.at[pl.ds((step - 1) * group, group), :],
                dst_ref=sum_recv.at[step - 1],
                send_sem=off_send_sem.at[step - 1],
                recv_sem=off_recv_sem.at[step - 1],
                device_id=(me_chan, off_peer(step)),
                device_id_type=MESH,
            )
        )
        moves_off[-1].start()
    total = out_ref[...]
    for step in range(1, half):
        moves_off[step - 1].wait_recv()
        total = total + sum_recv[step - 1].astype(jnp.float32)
    live = lax.broadcasted_iota(jnp.int32, (group, 1), 0) < limit_ref[0]
    out_ref[...] = jnp.where(live, total * (1.0 / math.sqrt(sample_count // 2)), 0.0)
    for move in moves:
        move.wait_send()
    swap.wait_send()
    for move in moves_off:
        move.wait_send()


def shards(traces, band_gain, pair_list, pair_count):
    chan_total = lax.axis_size("chan")
    owners = lax.axis_size("off")
    reach = chan_total // 4
    rows, sample_count = traces.shape
    bins = band_gain.shape[0]
    group = pair_list.shape[0] // owners
    half = owners // 2
    inner = sample_count // RADIX
    all_bins = bins * owners
    assert (inner // 2) % bins == 0 and bins % STEP == 0

    def const(value, dtype):
        return jnp.asarray(value, dtype=dtype)

    ic, isn = angle_table(np.arange(inner), np.arange(inner // 2), inner)
    oc, osn = angle_table(np.arange(RADIX), np.arange(all_bins), sample_count)
    lag_ids = np.arange(NLAG) - NLAG // 2
    cc, cs = angle_table(np.arange(0, all_bins, STEP), lag_ids, sample_count)
    fc, fs = angle_table(np.arange(STEP), lag_ids, sample_count)
    vmem = pl.BlockSpec(memory_space=pltpu.VMEM)
    smem = pl.BlockSpec(memory_space=pltpu.SMEM)
    dma = pltpu.SemaphoreType.DMA
    peers = max(1, half - 1)
    return pl.pallas_call(
        functools.partial(kernel, (chan_total, owners, reach)),
        out_shape=jax.ShapeDtypeStruct((group, NLAG), jnp.float32),
        in_specs=[vmem, vmem, vmem, smem] + [vmem] * 8,
        out_specs=vmem,
        scratch_shapes=[
            pltpu.VMEM((2 * reach + 1, rows, 2 * bins), jnp.bfloat16),
            pltpu.VMEM((2 * bins, NLAG), jnp.bfloat16),
            pltpu.VMEM((half * group, NLAG), jnp.bfloat16),
            pltpu.VMEM((half * group, NLAG), jnp.bfloat16),
            pltpu.VMEM((half, group, NLAG), jnp.float32),
            pltpu.VMEM((peers, group, NLAG), jnp.bfloat16),
            dma((2 * reach,)), dma((2 * reach,)),
            dma, dma,
            dma((peers,)), dma((peers,)),
        ],
        compiler_params=pltpu.CompilerParams(
            collective_id=0, has_side_effects=True, vmem_limit_bytes=48 * 1024 * 1024
        ),
        name="correlate",
    )(
        traces, band_gain.reshape(1, bins), pair_list, pair_count,
        const(ic, jnp.bfloat16), const(-isn, jnp.bfloat16),
        const(oc, jnp.float32), const(-osn, jnp.float32),
        const(cc, jnp.float32), const(cs, jnp.float32),
        const(fc, jnp.float32), const(fs, jnp.float32),
    )


def solution(mesh):
    placed = (P("chan", None), P("off"), P("chan", None), P(("chan", "off")))
    return jax.shard_map(
        shards, mesh=mesh, in_specs=placed, out_specs=P(("chan", "off"), None), check_vma=False
    )
```

```python
import functools
import math

import jax
import jax.numpy as jnp
import numpy as np
from jax import lax
from jax.experimental import pallas as pl
from jax.experimental.pallas import tpu as pltpu
from jax.sharding import PartitionSpec as P

NLAG = 1024
BAND = 64
RADIX = 4
LANES = 128
STEP = 64
MESH = pl.DeviceIdType.MESH


def angle_table(rows, cols, period):
    turns = np.mod(np.outer(rows, cols), period).astype(np.float64) * (2.0 * math.pi / period)
    return np.cos(turns), np.sin(turns)


def kernel(
    sizes,
    traces_hbm, gain_hbm, pairs_hbm, limit_hbm, inner_hbm, outer_hbm, coarse_hbm, fine_hbm,
    out_ref,
    traces_ref, gain_ref, pairs_ref, limit_ref, inner_ref, outer_ref, coarse_ref, fine_ref, slots, load_sem,
    table, inverse, part_send, part_recv, sum_send, sum_recv,
    chan_send_sem, chan_recv_sem, pair_send_sem, pair_recv_sem, off_send_sem, off_recv_sem,
):
    chan_total, owners, reach = sizes
    rows, sample_count = traces_ref.shape
    bins = gain_ref.shape[1]
    lags = out_ref.shape[1]
    group = out_ref.shape[0]
    half = owners // 2
    me_chan = lax.axis_index("chan")
    me_off = lax.axis_index("off")
    bin_lo = me_off * bins
    parity = lax.rem(me_off, 2)
    my_half = lax.div(me_off, 2)
    partner = me_off + 1 - 2 * parity

    def chan_peer(shift):
        return lax.rem(me_chan + shift + chan_total, chan_total)

    def off_peer(step):
        return 2 * lax.rem(my_half + step, half) + parity

    loads = [
        pltpu.make_async_copy(source, target, load_sem.at[i])
        for i, (source, target) in enumerate(
            (
                (traces_hbm, traces_ref), (inner_hbm, inner_ref), (outer_hbm, outer_ref), (gain_hbm, gain_ref),
                (fine_hbm, fine_ref), (coarse_hbm, coarse_ref), (pairs_hbm, pairs_ref), (limit_hbm, limit_ref),
            )
        )
    ]
    for load in loads:
        load.start()

    shifts = [s for d in range(1, reach + 1) for s in (d, -d)]
    barrier = pltpu.get_barrier_semaphore()
    for shift in shifts:
        pl.semaphore_signal(barrier, inc=1, device_id=(chan_peer(shift), me_off), device_id_type=MESH)
    pl.semaphore_signal(barrier, inc=1, device_id=(me_chan, partner), device_id_type=MESH)
    for step in range(1, half):
        pl.semaphore_signal(barrier, inc=1, device_id=(me_chan, off_peer(step)), device_id_type=MESH)

    inner = sample_count // RADIX
    chunk = RADIX * LANES
    chunks = sample_count // chunk
    odd_half = lax.rem(lax.div(bin_lo, inner // 2), 2)
    src = lax.broadcasted_iota(jnp.int32, (chunk, chunk), 0)
    dst = lax.broadcasted_iota(jnp.int32, (chunk, chunk), 1)
    lane = lax.rem(dst, LANES)
    wanted = RADIX * lane + lax.div(dst, LANES)
    flip = 1.0 - 2.0 * (lax.rem(lane, 2) * odd_half).astype(jnp.float32)
    spread = jnp.where(src == wanted, flip, 0.0).astype(jnp.bfloat16)
    loads[0].wait()
    stacked = jnp.concatenate([traces_ref[:, c * chunk:(c + 1) * chunk] for c in range(chunks)], axis=0)
    split = jnp.dot(stacked, spread, preferred_element_type=jnp.float32).astype(jnp.bfloat16)
    by_residue = jnp.concatenate(
        [
            jnp.concatenate(
                [split[c * rows:(c + 1) * rows, r * LANES:(r + 1) * LANES] for c in range(chunks)], axis=1
            )
            for r in range(RADIX)
        ],
        axis=0,
    )
    col_lo = pl.multiple_of(lax.rem(bin_lo, inner // 2), LANES)
    loads[1].wait()
    in_re = jnp.dot(by_residue, inner_ref[0, :, pl.ds(col_lo, bins)], preferred_element_type=jnp.float32)
    in_im = jnp.dot(by_residue, inner_ref[1, :, pl.ds(col_lo, bins)], preferred_element_type=jnp.float32)
    tw_lo = pl.multiple_of(bin_lo, LANES)
    loads[2].wait()
    loads[3].wait()
    real_part = in_re[:rows]
    imag_part = in_im[:rows]
    for r in range(1, RADIX):
        tc = outer_ref[r:r + 1, pl.ds(tw_lo, bins)]
        ts = outer_ref[RADIX + r:RADIX + r + 1, pl.ds(tw_lo, bins)]
        a = in_re[r * rows:(r + 1) * rows]
        b = in_im[r * rows:(r + 1) * rows]
        real_part += a * tc - b * ts
        imag_part += a * ts + b * tc

    power = real_part * real_part + imag_part * imag_part
    high = power.astype(jnp.bfloat16)
    low = (power - high.astype(jnp.float32)).astype(jnp.bfloat16)
    band_a = lax.div(lax.broadcasted_iota(jnp.int32, (bins, bins), 0), BAND)
    band_b = lax.div(lax.broadcasted_iota(jnp.int32, (bins, bins), 1), BAND)
    mean_of = jnp.where(band_a == band_b, 1.0 / BAND, 0.0).astype(jnp.bfloat16)
    mean = jnp.dot(high, mean_of, preferred_element_type=jnp.float32) + jnp.dot(
        low, mean_of, preferred_element_type=jnp.float32
    )
    scale = lax.rsqrt(mean + 1e-06) * gain_ref[...]
    own = table.at[reach]
    own[:, :bins] = (real_part * scale).astype(jnp.bfloat16)
    own[:, bins:] = (imag_part * scale).astype(jnp.bfloat16)

    pl.semaphore_wait(barrier, len(shifts) + half)

    moves = []
    for i, shift in enumerate(shifts):
        moves.append(
            pltpu.make_async_remote_copy(
                src_ref=own,
                dst_ref=table.at[reach - shift],
                send_sem=chan_send_sem.at[i],
                recv_sem=chan_recv_sem.at[i],
                device_id=(chan_peer(shift), me_off),
                device_id_type=MESH,
            )
        )
    for move in reversed(moves):
        move.start()

    for load in loads[4:]:
        load.wait()
    slots[...] = jnp.transpose(pairs_ref[...])
    row_lo = lax.div(bin_lo, STEP)

    def fill(a, carry):
        cc = coarse_ref[0, pl.ds(row_lo + a, 1), :]
        cs = coarse_ref[1, pl.ds(row_lo + a, 1), :]
        fc = fine_ref[0]
        fs = fine_ref[1]
        at = pl.multiple_of(a * STEP, STEP)
        inverse[pl.ds(at, STEP), :] = (cc * fc - cs * fs).astype(jnp.bfloat16)
        inverse[pl.ds(bins + at, STEP), :] = (-(cs * fc + cc * fs)).astype(jnp.bfloat16)
        return carry

    lax.fori_loop(0, bins // STEP, fill, 0)

    for move in moves:
        move.wait_recv()

    span = (2 * reach + 1) * rows
    chan_a = me_chan * rows + lax.broadcasted_iota(jnp.int32, (1, rows), 1)
    chan_b = (me_chan - reach) * rows + lax.broadcasted_iota(jnp.int32, (1, span), 1)
    chan_b = jnp.where(chan_b < 0, chan_b + chan_total * rows, chan_b)
    chan_b = jnp.where(chan_b >= chan_total * rows, chan_b - chan_total * rows, chan_b)

    def lag_rows(par):
        pairs = jnp.concatenate(
            [slots[pl.ds(pl.multiple_of((2 * h + par) * group, group), group), :] for h in range(half)], axis=0
        )
        pick_a = jnp.where(pairs[:, 0:1] == chan_a, 1.0, 0.0).astype(jnp.bfloat16)
        pick_b = jnp.where(pairs[:, 1:2] == chan_b, 1.0, 0.0).astype(jnp.bfloat16)
        left = jnp.dot(pick_a, own[...], preferred_element_type=jnp.float32)
        right = jnp.dot(
            pick_b, table[...].reshape(span, 2 * bins), preferred_element_type=jnp.float32
        )
        la, lb = left[:, :bins], left[:, bins:]
        ra, rb = right[:, :bins], right[:, bins:]
        cross = jnp.concatenate([la * ra + lb * rb, la * rb - lb * ra], axis=1).astype(jnp.bfloat16)
        return jnp.dot(cross, inverse[...], preferred_element_type=jnp.float32)

    part_send[...] = lag_rows(1 - parity).astype(part_send.dtype)
    swap = pltpu.make_async_remote_copy(
        src_ref=part_send,
        dst_ref=part_recv,
        send_sem=pair_send_sem,
        recv_sem=pair_recv_sem,
        device_id=(me_chan, partner),
        device_id_type=MESH,
    )
    swap.start()
    mine = lag_rows(parity)
    swap.wait_recv()
    mine = mine + part_recv[...].astype(jnp.float32)
    for h in range(half):
        sum_send[h] = mine[h * group:(h + 1) * group]
    narrow = sum_recv.dtype
    sends = []
    for step in range(1, half):
        slot = lax.rem(my_half + step, half)
        part_send_slot = sum_send.at[slot]
        sends.append(part_send_slot)
    out_ref[...] = sum_send[my_half]
    moves_off = []
    stage = part_recv
    for step in range(1, half):
        slot = lax.rem(my_half + step, half)
        stage[pl.ds((step - 1) * group, group), :] = sum_send[slot].astype(narrow)
        moves_off.append(
            pltpu.make_async_remote_copy(
                src_ref=stage.at[pl.ds((step - 1) * group, group), :],
                dst_ref=sum_recv.at[step - 1],
                send_sem=off_send_sem.at[step - 1],
                recv_sem=off_recv_sem.at[step - 1],
                device_id=(me_chan, off_peer(step)),
                device_id_type=MESH,
            )
        )
        moves_off[-1].start()
    total = out_ref[...]
    for step in range(1, half):
        moves_off[step - 1].wait_recv()
        total = total + sum_recv[step - 1].astype(jnp.float32)
    live = lax.broadcasted_iota(jnp.int32, (group, 1), 0) < limit_ref[0]
    out_ref[...] = jnp.where(live, total * (1.0 / math.sqrt(sample_count // 2)), 0.0)
    for move in moves:
        move.wait_send()
    swap.wait_send()
    for move in moves_off:
        move.wait_send()


def shards(traces, band_gain, pair_list, pair_count):
    chan_total = lax.axis_size("chan")
    owners = lax.axis_size("off")
    reach = chan_total // 4
    rows, sample_count = traces.shape
    bins = band_gain.shape[0]
    group = pair_list.shape[0] // owners
    half = owners // 2
    inner = sample_count // RADIX
    all_bins = bins * owners
    assert (inner // 2) % bins == 0 and bins % STEP == 0

    def const(value, dtype):
        return jnp.asarray(value, dtype=dtype)

    ic, isn = angle_table(np.arange(inner), np.arange(inner // 2), inner)
    oc, osn = angle_table(np.arange(RADIX), np.arange(all_bins), sample_count)
    lag_ids = np.arange(NLAG) - NLAG // 2
    cc, cs = angle_table(np.arange(0, all_bins, STEP), lag_ids, sample_count)
    fc, fs = angle_table(np.arange(STEP), lag_ids, sample_count)
    vmem = pl.BlockSpec(memory_space=pltpu.VMEM)
    hbm = pl.BlockSpec(memory_space=pltpu.HBM)
    dma = pltpu.SemaphoreType.DMA
    peers = max(1, half - 1)
    operands = (
        traces, band_gain.reshape(1, bins), pair_list.T, pair_count,
        const(np.stack([ic, -isn]), jnp.bfloat16),
        const(np.concatenate([oc, -osn]), jnp.float32),
        const(np.stack([cc, cs]), jnp.float32),
        const(np.stack([fc, fs]), jnp.float32),
    )
    return pl.pallas_call(
        functools.partial(kernel, (chan_total, owners, reach)),
        out_shape=jax.ShapeDtypeStruct((group, NLAG), jnp.float32),
        in_specs=[hbm] * 8,
        out_specs=vmem,
        scratch_shapes=[
            *[(pltpu.SMEM if x.shape == (1,) else pltpu.VMEM)(x.shape, x.dtype) for x in operands],
            pltpu.VMEM(pair_list.shape, jnp.int32), dma((len(operands),)),
            pltpu.VMEM((2 * reach + 1, rows, 2 * bins), jnp.bfloat16),
            pltpu.VMEM((2 * bins, NLAG), jnp.bfloat16),
            pltpu.VMEM((half * group, NLAG), jnp.bfloat16),
            pltpu.VMEM((half * group, NLAG), jnp.bfloat16),
            pltpu.VMEM((half, group, NLAG), jnp.float32),
            pltpu.VMEM((peers, group, NLAG), jnp.bfloat16),
            dma((2 * reach,)), dma((2 * reach,)),
            dma, dma,
            dma((peers,)), dma((peers,)),
        ],
        compiler_params=pltpu.CompilerParams(
            collective_id=0, has_side_effects=True, vmem_limit_bytes=60 * 1024 * 1024
        ),
        name="correlate",
    )(*operands)


def solution(mesh):
    placed = (P("chan", None), P("off"), P("chan", None), P(("chan", "off")))
    return jax.shard_map(
        shards, mesh=mesh, in_specs=placed, out_specs=P(("chan", "off"), None), check_vma=False
    )
```

```python
import functools
import math

import jax
import jax.numpy as jnp
import numpy as np
from jax import lax
from jax.experimental import pallas as pl
from jax.experimental.pallas import tpu as pltpu
from jax.sharding import PartitionSpec as P

NLAG = 1024
BAND = 64
RADIX = 4
LANES = 128
STEP = 64
MESH = pl.DeviceIdType.MESH


def angle_table(rows, cols, period):
    turns = np.mod(np.outer(rows, cols), period).astype(np.float64) * (2.0 * math.pi / period)
    return np.cos(turns), np.sin(turns)


def kernel(
    sizes,
    traces_hbm, gain_hbm, pairs_hbm, inner_hbm, outer_hbm, coarse_hbm, fine_hbm,
    out_ref,
    traces_ref, gain_ref, pairs_ref, inner_ref, outer_ref, coarse_ref, fine_ref, slots, load_sem,
    table, inverse, total, swap_send, swap_recv, sum_send, sum_recv,
    chan_send_sem, chan_recv_sem, swap_send_sem, swap_recv_sem, off_send_sem, off_recv_sem,
):
    chan_total, owners, reach = sizes
    rows, sample_count = traces_ref.shape
    bins = gain_ref.shape[1]
    group = out_ref.shape[0]
    half = owners // 2
    pieces = bins // LANES
    me_chan = lax.axis_index("chan")
    me_off = lax.axis_index("off")
    bin_lo = me_off * bins
    parity = lax.rem(me_off, 2)
    my_half = lax.div(me_off, 2)
    partner = me_off + 1 - 2 * parity

    def chan_peer(shift):
        return lax.rem(me_chan + shift + chan_total, chan_total)

    def off_peer(step):
        return 2 * lax.rem(my_half + step, half) + parity

    loads = [
        pltpu.make_async_copy(source, target, load_sem.at[i])
        for i, (source, target) in enumerate(
            (
                (traces_hbm, traces_ref), (inner_hbm, inner_ref), (outer_hbm, outer_ref), (gain_hbm, gain_ref),
                (fine_hbm, fine_ref), (coarse_hbm, coarse_ref), (pairs_hbm, pairs_ref),
            )
        )
    ]
    for load in loads:
        load.start()

    shifts = [s for d in range(reach, 0, -1) for s in (d, -d)]
    barrier = pltpu.get_barrier_semaphore()
    for shift in shifts:
        pl.semaphore_signal(barrier, inc=1, device_id=(chan_peer(shift), me_off), device_id_type=MESH)
    pl.semaphore_signal(barrier, inc=1, device_id=(me_chan, partner), device_id_type=MESH)
    for step in range(1, half):
        pl.semaphore_signal(barrier, inc=1, device_id=(me_chan, off_peer(step)), device_id_type=MESH)

    inner = sample_count // RADIX
    chunk = RADIX * LANES
    chunks = sample_count // chunk
    odd_half = lax.rem(lax.div(bin_lo, inner // 2), 2)
    src = lax.broadcasted_iota(jnp.int32, (chunk, chunk), 0)
    dst = lax.broadcasted_iota(jnp.int32, (chunk, chunk), 1)
    lane = lax.rem(dst, LANES)
    wanted = RADIX * lane + lax.div(dst, LANES)
    flip = 1.0 - 2.0 * (lax.rem(lane, 2) * odd_half).astype(jnp.float32)
    spread = jnp.where(src == wanted, flip, 0.0).astype(jnp.bfloat16)
    band_a = lax.div(lax.broadcasted_iota(jnp.int32, (LANES, LANES), 0), BAND)
    band_b = lax.div(lax.broadcasted_iota(jnp.int32, (LANES, LANES), 1), BAND)
    mean_of = jnp.where(band_a == band_b, 1.0 / BAND, 0.0).astype(jnp.bfloat16)
    loads[0].wait()
    stacked = jnp.concatenate([traces_ref[:, c * chunk:(c + 1) * chunk] for c in range(chunks)], axis=0)
    split = jnp.dot(stacked, spread, preferred_element_type=jnp.float32).astype(jnp.bfloat16)
    by_residue = jnp.concatenate(
        [
            jnp.concatenate(
                [split[c * rows:(c + 1) * rows, r * LANES:(r + 1) * LANES] for c in range(chunks)], axis=1
            )
            for r in range(RADIX)
        ],
        axis=0,
    )
    for load in loads[1:4]:
        load.wait()
    col_lo = lax.rem(bin_lo, inner // 2)

    moves = []
    for q in range(pieces):
        at = pl.multiple_of(2 * (col_lo + q * LANES), LANES)
        part = jnp.dot(by_residue, inner_ref[:, pl.ds(at, 2 * LANES)], preferred_element_type=jnp.float32)
        real_part = part[:rows, :LANES]
        imag_part = part[:rows, LANES:]
        tw = pl.ds(pl.multiple_of(bin_lo + q * LANES, LANES), LANES)
        for r in range(1, RADIX):
            tc = outer_ref[r:r + 1, tw]
            ts = outer_ref[RADIX + r:RADIX + r + 1, tw]
            a = part[r * rows:(r + 1) * rows, :LANES]
            b = part[r * rows:(r + 1) * rows, LANES:]
            real_part += a * tc - b * ts
            imag_part += a * ts + b * tc
        power = real_part * real_part + imag_part * imag_part
        high = power.astype(jnp.bfloat16)
        low = (power - high.astype(jnp.float32)).astype(jnp.bfloat16)
        mean = jnp.dot(high, mean_of, preferred_element_type=jnp.float32) + jnp.dot(
            low, mean_of, preferred_element_type=jnp.float32
        )
        scale = lax.rsqrt(mean + 1e-06) * gain_ref[:, q * LANES:(q + 1) * LANES]
        table[q, reach, :, :LANES] = (real_part * scale).astype(jnp.bfloat16)
        table[q, reach, :, LANES:] = (imag_part * scale).astype(jnp.bfloat16)
        if q == 0:
            pl.semaphore_wait(barrier, len(shifts) + half)
        for i, shift in enumerate(shifts):
            move = pltpu.make_async_remote_copy(
                src_ref=table.at[q, reach],
                dst_ref=table.at[q, reach - shift],
                send_sem=chan_send_sem.at[q, i],
                recv_sem=chan_recv_sem.at[q, i],
                device_id=(chan_peer(shift), me_off),
                device_id_type=MESH,
            )
            move.start()
            moves.append(move)

    for load in loads[4:]:
        load.wait()
    slots[...] = jnp.transpose(pairs_ref[...])
    row_lo = lax.div(bin_lo, STEP)
    per = LANES // STEP

    def fill(a, carry):
        cc = coarse_ref[0, pl.ds(row_lo + a, 1), :]
        cs = coarse_ref[1, pl.ds(row_lo + a, 1), :]
        fc = fine_ref[0]
        fs = fine_ref[1]
        at = pl.multiple_of(a // per * 2 * LANES + a % per * STEP, STEP)
        inverse[pl.ds(at, STEP), :] = (cc * fc - cs * fs).astype(jnp.bfloat16)
        inverse[pl.ds(LANES + at, STEP), :] = (-(cs * fc + cc * fs)).astype(jnp.bfloat16)
        return carry

    lax.fori_loop(0, bins // STEP, fill, 0)

    span = (2 * reach + 1) * rows
    chan_a = me_chan * rows + lax.broadcasted_iota(jnp.int32, (1, rows), 1)
    chan_b = (me_chan - reach) * rows + lax.broadcasted_iota(jnp.int32, (1, span), 1)
    chan_b = jnp.where(chan_b < 0, chan_b + chan_total * rows, chan_b)
    chan_b = jnp.where(chan_b >= chan_total * rows, chan_b - chan_total * rows, chan_b)
    far = (half - 1) * group
    order = [off_peer(s) + 1 - 2 * parity for s in range(1, half)] + [off_peer(s) for s in range(1, half)]
    order += [partner, me_off]
    pairs = jnp.concatenate(
        [slots[pl.ds(pl.multiple_of(o * group, group), group), :] for o in order], axis=0
    )
    pick_a = jnp.where(pairs[:, 0:1] == chan_a, 1.0, 0.0).astype(jnp.bfloat16)
    pick_b = jnp.where(pairs[:, 1:2] == chan_b, 1.0, 0.0).astype(jnp.bfloat16)

    def product(q, lo, hi):
        left = jnp.dot(pick_a[lo:hi], table[q, reach], preferred_element_type=jnp.float32)
        right = jnp.dot(
            pick_b[lo:hi], table[q].reshape(span, 2 * LANES), preferred_element_type=jnp.float32
        )
        la, lb = left[:, :LANES], left[:, LANES:]
        ra, rb = right[:, :LANES], right[:, LANES:]
        cross = jnp.concatenate([la * ra + lb * rb, la * rb - lb * ra], axis=1).astype(jnp.bfloat16)
        return jnp.dot(
            cross, inverse[q * 2 * LANES:(q + 1) * 2 * LANES, :], preferred_element_type=jnp.float32
        )

    def swap(index, lo, count):
        copy = pltpu.make_async_remote_copy(
            src_ref=swap_send.at[pl.ds(lo, count), :],
            dst_ref=swap_recv.at[pl.ds(lo, count), :],
            send_sem=swap_send_sem.at[index],
            recv_sem=swap_recv_sem.at[index],
            device_id=(me_chan, partner),
            device_id_type=MESH,
        )
        copy.start()
        return copy

    everything = 2 * far + 2 * group
    for q in range(pieces - 1):
        for move in moves[q * len(shifts):(q + 1) * len(shifts)]:
            move.wait_recv()
        if q == 0:
            total[...] = product(q, 0, everything)
        else:
            total[...] += product(q, 0, everything)
    for move in moves[(pieces - 1) * len(shifts):]:
        move.wait_recv()

    def last(lo, hi):
        value = product(pieces - 1, lo, hi)
        return value + total[lo:hi, :] if pieces > 1 else value

    outer_rows = last(0, 2 * far)
    swap_send[:far, :] = outer_rows[:far].astype(swap_send.dtype)
    swap_far = swap(0, 0, far)
    total[far:2 * far, :] = outer_rows[far:]
    near_rows = last(2 * far, everything)
    swap_send[far:, :] = near_rows[:group].astype(swap_send.dtype)
    swap_near = swap(1, far, group)
    out_ref[...] = near_rows[group:]
    swap_far.wait_recv()
    sends = []
    for step in range(1, half):
        lo = (step - 1) * group
        sum_send[lo:lo + group, :] = (
            total[far + lo:far + lo + group, :] + swap_recv[lo:lo + group, :].astype(jnp.float32)
        ).astype(sum_send.dtype)
        send = pltpu.make_async_remote_copy(
            src_ref=sum_send.at[pl.ds(lo, group), :],
            dst_ref=sum_recv.at[pl.ds(lo, group), :],
            send_sem=off_send_sem.at[step - 1],
            recv_sem=off_recv_sem.at[step - 1],
            device_id=(me_chan, off_peer(step)),
            device_id_type=MESH,
        )
        send.start()
        sends.append(send)
    swap_near.wait_recv()
    result = out_ref[...] + swap_recv[far:, :].astype(jnp.float32)
    for step in range(1, half):
        sends[step - 1].wait_recv()
        result += sum_recv[(step - 1) * group:step * group, :].astype(jnp.float32)
    out_ref[...] = result
    for copy in moves + [swap_far, swap_near] + sends:
        copy.wait_send()


def shards(traces, band_gain, pair_list, pair_count):
    chan_total = lax.axis_size("chan")
    owners = lax.axis_size("off")
    reach = chan_total // 4
    rows, sample_count = traces.shape
    bins = band_gain.shape[0]
    group = pair_list.shape[0] // owners
    half = owners // 2
    inner = sample_count // RADIX
    all_bins = bins * owners
    assert (inner // 2) % bins == 0 and bins % LANES == 0 and half > 1

    def const(value, dtype):
        return jnp.asarray(value, dtype=dtype)

    ic, isn = angle_table(np.arange(inner), np.arange(inner // 2), inner)
    oc, osn = angle_table(np.arange(RADIX), np.arange(all_bins), sample_count)
    lag_ids = np.arange(NLAG) - NLAG // 2
    cc, cs = angle_table(np.arange(0, all_bins, STEP), lag_ids, sample_count)
    fc, fs = angle_table(np.arange(STEP), lag_ids, sample_count)
    vmem = pl.BlockSpec(memory_space=pltpu.VMEM)
    hbm = pl.BlockSpec(memory_space=pltpu.HBM)
    dma = pltpu.SemaphoreType.DMA
    peers = max(1, half - 1)
    operands = (
        traces, band_gain.reshape(1, bins), pair_list.T,
        const(np.stack([ic.reshape(inner, -1, LANES), -isn.reshape(inner, -1, LANES)], axis=2).reshape(inner, inner), jnp.bfloat16),
        const(np.concatenate([oc, -osn]), jnp.float32),
        const(np.stack([cc, cs]), jnp.float32),
        const(np.stack([fc, fs]), jnp.float32),
    )
    lagsum = pl.pallas_call(
        functools.partial(kernel, (chan_total, owners, reach)),
        out_shape=jax.ShapeDtypeStruct((group, NLAG), jnp.float32),
        in_specs=[hbm] * len(operands),
        out_specs=vmem,
        scratch_shapes=[
            *[pltpu.VMEM(x.shape, x.dtype) for x in operands],
            pltpu.VMEM(pair_list.shape, jnp.int32), dma((len(operands),)),
            pltpu.VMEM((bins // LANES, 2 * reach + 1, rows, 2 * LANES), jnp.bfloat16),
            pltpu.VMEM((2 * bins, NLAG), jnp.bfloat16),
            pltpu.VMEM((owners * group, NLAG), jnp.float32),
            pltpu.VMEM((half * group, NLAG), jnp.bfloat16),
            pltpu.VMEM((half * group, NLAG), jnp.bfloat16),
            pltpu.VMEM((peers * group, NLAG), jnp.bfloat16),
            pltpu.VMEM((peers * group, NLAG), jnp.bfloat16),
            dma((bins // LANES, 2 * reach)), dma((bins // LANES, 2 * reach)),
            dma((2,)), dma((2,)),
            dma((peers,)), dma((peers,)),
        ],
        compiler_params=pltpu.CompilerParams(
            collective_id=0, has_side_effects=True, vmem_limit_bytes=60 * 1024 * 1024
        ),
        name="correlate",
    )(*operands)
    live = jnp.arange(group, dtype=jnp.int32)[:, None] < pair_count[0]
    return jnp.where(live, lagsum * (1.0 / math.sqrt(sample_count // 2)), 0.0)


def solution(mesh):
    placed = (P("chan", None), P("off"), P("chan", None), P(("chan", "off")))
    return jax.shard_map(
        shards, mesh=mesh, in_specs=placed, out_specs=P(("chan", "off"), None), check_vma=False
    )
```

```python
import functools
import math

import jax
import jax.numpy as jnp
import numpy as np
from jax import lax
from jax.experimental import pallas as pl
from jax.experimental.pallas import tpu as pltpu
from jax.sharding import PartitionSpec as P

NLAG = 1024
BAND = 64
RADIX = 4
LANES = 128
STEP = 64
VMEM_MIB = 58
MESH = pl.DeviceIdType.MESH


def angle_table(rows, cols, period):
    turns = np.mod(np.outer(rows, cols), period).astype(np.float64) * (2.0 * math.pi / period)
    return np.cos(turns), np.sin(turns)


def kernel(
    sizes,
    traces_hbm, gain_hbm, pairs_hbm, limit_hbm, inner_hbm, outer_hbm, coarse_hbm, fine_hbm,
    out_ref,
    traces_ref, gain_ref, pairs_ref, limit_ref, inner_ref, outer_ref, coarse_ref, fine_ref, slots, load_sem,
    table, inverse, total, swap_send, swap_recv, sum_send, sum_recv,
    chan_send_sem, chan_recv_sem, swap_send_sem, swap_recv_sem, off_send_sem, off_recv_sem,
):
    chan_total, owners, reach = sizes
    rows, sample_count = traces_ref.shape
    bins = gain_ref.shape[1]
    group = out_ref.shape[0]
    half = owners // 2
    pieces = bins // LANES
    me_chan = lax.axis_index("chan")
    me_off = lax.axis_index("off")
    bin_lo = me_off * bins
    parity = lax.rem(me_off, 2)
    my_half = lax.div(me_off, 2)
    partner = me_off + 1 - 2 * parity

    def chan_peer(shift):
        return lax.rem(me_chan + shift + chan_total, chan_total)

    def off_peer(step):
        return 2 * lax.rem(my_half + step, half) + parity

    loads = [
        pltpu.make_async_copy(source, target, load_sem.at[i])
        for i, (source, target) in enumerate(
            (
                (traces_hbm, traces_ref), (inner_hbm, inner_ref), (outer_hbm, outer_ref), (gain_hbm, gain_ref),
                (fine_hbm, fine_ref), (coarse_hbm, coarse_ref), (pairs_hbm, pairs_ref), (limit_hbm, limit_ref),
            )
        )
    ]
    for load in loads:
        load.start()

    shifts = [s for d in range(reach, 0, -1) for s in (d, -d)]
    relayed = pieces - 1 if reach == 2 and chan_total % 2 == 0 else 0
    side = 1 - 2 * lax.rem(me_chan, 2)
    barrier = pltpu.get_barrier_semaphore()
    for shift in shifts:
        pl.semaphore_signal(barrier, inc=1, device_id=(chan_peer(shift), me_off), device_id_type=MESH)
    pl.semaphore_signal(barrier, inc=1, device_id=(me_chan, partner), device_id_type=MESH)
    for step in range(1, half):
        pl.semaphore_signal(barrier, inc=1, device_id=(me_chan, off_peer(step)), device_id_type=MESH)

    inner = sample_count // RADIX
    chunk = RADIX * LANES
    chunks = sample_count // chunk
    odd_half = lax.rem(lax.div(bin_lo, inner // 2), 2)
    src = lax.broadcasted_iota(jnp.int32, (chunk, chunk), 0)
    dst = lax.broadcasted_iota(jnp.int32, (1, chunk), 1)
    lane = jnp.bitwise_and(dst, LANES - 1)
    wanted = RADIX * lane + jnp.right_shift(dst, LANES.bit_length() - 1)
    flip = 1.0 - 2.0 * (jnp.bitwise_and(lane, 1) * odd_half).astype(jnp.float32)
    spread = jnp.where(src == wanted, flip, 0.0).astype(jnp.bfloat16)
    band_a = jnp.right_shift(lax.broadcasted_iota(jnp.int32, (LANES, LANES), 0), BAND.bit_length() - 1)
    band_b = jnp.right_shift(lax.broadcasted_iota(jnp.int32, (LANES, LANES), 1), BAND.bit_length() - 1)
    mean_of = jnp.where(band_a == band_b, 1.0 / BAND, 0.0).astype(jnp.bfloat16)
    loads[0].wait()
    stacked = jnp.concatenate([traces_ref[:, c * chunk:(c + 1) * chunk] for c in range(chunks)], axis=0)
    split = jnp.dot(stacked, spread, preferred_element_type=jnp.float32).astype(jnp.bfloat16)
    by_residue = jnp.concatenate(
        [
            jnp.concatenate(
                [split[c * rows:(c + 1) * rows, r * LANES:(r + 1) * LANES] for c in range(chunks)], axis=1
            )
            for r in range(RADIX)
        ],
        axis=0,
    )
    for load in loads[1:4]:
        load.wait()
    col_lo = lax.rem(bin_lo, inner // 2)

    def send_block(q, i, source, target, shift):
        move = pltpu.make_async_remote_copy(
            src_ref=table.at[q, source],
            dst_ref=table.at[q, target],
            send_sem=chan_send_sem.at[q, i],
            recv_sem=chan_recv_sem.at[q, i],
            device_id=(chan_peer(shift), me_off),
            device_id_type=MESH,
        )
        move.start()
        return move

    moves = []
    for q in range(pieces):
        at = pl.multiple_of(2 * (col_lo + q * LANES), LANES)
        part = jnp.dot(by_residue, inner_ref[:, pl.ds(at, 2 * LANES)], preferred_element_type=jnp.float32)
        real_part = part[:rows, :LANES]
        imag_part = part[:rows, LANES:]
        tw = pl.ds(pl.multiple_of(bin_lo + q * LANES, LANES), LANES)
        for r in range(1, RADIX):
            tc = outer_ref[r:r + 1, tw]
            ts = outer_ref[RADIX + r:RADIX + r + 1, tw]
            a = part[r * rows:(r + 1) * rows, :LANES]
            b = part[r * rows:(r + 1) * rows, LANES:]
            real_part += a * tc - b * ts
            imag_part += a * ts + b * tc
        power = real_part * real_part + imag_part * imag_part
        high = power.astype(jnp.bfloat16)
        low = (power - high.astype(jnp.float32)).astype(jnp.bfloat16)
        mean = jnp.dot(high, mean_of, preferred_element_type=jnp.float32) + jnp.dot(
            low, mean_of, preferred_element_type=jnp.float32
        )
        scale = lax.rsqrt(mean + 1e-06) * gain_ref[:, q * LANES:(q + 1) * LANES]
        table[q, reach, :, :LANES] = (real_part * scale).astype(jnp.bfloat16)
        table[q, reach, :, LANES:] = (imag_part * scale).astype(jnp.bfloat16)
        if q == 0:
            pl.semaphore_wait(barrier, len(shifts) + half)
        moves.append([])
        for i, shift in enumerate(shifts):
            near = q < relayed and abs(shift) == 1
            if near and shift == -1:
                continue
            if near:
                shift = side
            moves[q].append(send_block(q, i, reach, reach - shift, shift))

    for load in loads[4:]:
        load.wait()
    slots[...] = jnp.transpose(pairs_ref[...])
    row_lo = lax.div(bin_lo, STEP)
    per = LANES // STEP

    def fill(a, carry):
        cc = coarse_ref[0, pl.ds(row_lo + a, 1), :]
        cs = coarse_ref[1, pl.ds(row_lo + a, 1), :]
        fc = fine_ref[0]
        fs = fine_ref[1]
        at = pl.multiple_of(a // per * 2 * LANES + a % per * STEP, STEP)
        inverse[pl.ds(at, STEP), :] = (cc * fc - cs * fs).astype(jnp.bfloat16)
        inverse[pl.ds(LANES + at, STEP), :] = (-(cs * fc + cc * fs)).astype(jnp.bfloat16)
        return carry

    lax.fori_loop(0, bins // STEP, fill, 0)

    span = (2 * reach + 1) * rows
    chan_a = me_chan * rows + lax.broadcasted_iota(jnp.int32, (1, rows), 1)
    chan_b = (me_chan - reach) * rows + lax.broadcasted_iota(jnp.int32, (1, span), 1)
    chan_b = jnp.where(chan_b < 0, chan_b + chan_total * rows, chan_b)
    chan_b = jnp.where(chan_b >= chan_total * rows, chan_b - chan_total * rows, chan_b)
    far = (half - 1) * group
    order = [off_peer(s) + 1 - 2 * parity for s in range(1, half)] + [off_peer(s) for s in range(1, half)]
    order += [partner, me_off]
    pairs = jnp.concatenate(
        [slots[pl.ds(pl.multiple_of(o * group, group), group), :] for o in order], axis=0
    )
    pick_a = jnp.where(pairs[:, 0:1] == chan_a, 1.0, 0.0).astype(jnp.bfloat16)
    pick_b = jnp.where(pairs[:, 1:2] == chan_b, 1.0, 0.0).astype(jnp.bfloat16)

    def product(q, lo, hi):
        left = jnp.dot(pick_a[lo:hi], table[q, reach], preferred_element_type=jnp.float32)
        right = jnp.dot(
            pick_b[lo:hi], table[q].reshape(span, 2 * LANES), preferred_element_type=jnp.float32
        )
        la, lb = left[:, :LANES], left[:, LANES:]
        ra, rb = right[:, :LANES], right[:, LANES:]
        cross = jnp.concatenate([la * ra + lb * rb, la * rb - lb * ra], axis=1).astype(jnp.bfloat16)
        return jnp.dot(
            cross, inverse[q * 2 * LANES:(q + 1) * 2 * LANES, :], preferred_element_type=jnp.float32
        )

    def swap(index, lo, count):
        copy = pltpu.make_async_remote_copy(
            src_ref=swap_send.at[pl.ds(lo, count), :],
            dst_ref=swap_recv.at[pl.ds(lo, count), :],
            send_sem=swap_send_sem.at[index],
            recv_sem=swap_recv_sem.at[index],
            device_id=(me_chan, partner),
            device_id_type=MESH,
        )
        copy.start()
        return copy

    everything = 2 * far + 2 * group
    for q in range(relayed):
        for move in moves[q][:2]:
            move.wait_recv()
        moves[q].append(send_block(q, len(shifts) - 1, reach + 2 * side, reach + side, side))
    for q in range(pieces - 1):
        for move in moves[q][2 if q < relayed else 0:]:
            move.wait_recv()
        if q == 0:
            total[...] = product(q, 0, everything)
        else:
            total[...] += product(q, 0, everything)
    for move in moves[pieces - 1]:
        move.wait_recv()

    def last(lo, hi):
        value = product(pieces - 1, lo, hi)
        return value + total[lo:hi, :] if pieces > 1 else value

    outer_rows = last(0, 2 * far)
    swap_send[:far, :] = outer_rows[:far].astype(swap_send.dtype)
    swap_far = swap(0, 0, far)
    total[far:2 * far, :] = outer_rows[far:]
    near_rows = last(2 * far, everything)
    swap_send[far:, :] = near_rows[:group].astype(swap_send.dtype)
    swap_near = swap(1, far, group)
    out_ref[...] = near_rows[group:]
    swap_far.wait_recv()
    sends = []
    for step in range(1, half):
        lo = (step - 1) * group
        sum_send[lo:lo + group, :] = (
            total[far + lo:far + lo + group, :] + swap_recv[lo:lo + group, :].astype(jnp.float32)
        ).astype(sum_send.dtype)
        send = pltpu.make_async_remote_copy(
            src_ref=sum_send.at[pl.ds(lo, group), :],
            dst_ref=sum_recv.at[pl.ds(lo, group), :],
            send_sem=off_send_sem.at[step - 1],
            recv_sem=off_recv_sem.at[step - 1],
            device_id=(me_chan, off_peer(step)),
            device_id_type=MESH,
        )
        send.start()
        sends.append(send)
    swap_near.wait_recv()
    result = out_ref[...] + swap_recv[far:, :].astype(jnp.float32)
    for step in range(1, half):
        sends[step - 1].wait_recv()
        result += sum_recv[(step - 1) * group:step * group, :].astype(jnp.float32)
    live = lax.broadcasted_iota(jnp.int32, (group, 1), 0) < limit_ref[...]
    out_ref[...] = jnp.where(live, result * (1.0 / math.sqrt(sample_count // 2)), 0.0)
    for copy in [move for piece in moves for move in piece] + [swap_far, swap_near] + sends:
        copy.wait_send()


def shards(traces, band_gain, pair_list, pair_count):
    chan_total = lax.axis_size("chan")
    owners = lax.axis_size("off")
    reach = chan_total // 4
    rows, sample_count = traces.shape
    bins = band_gain.shape[0]
    group = pair_list.shape[0] // owners
    half = owners // 2
    inner = sample_count // RADIX
    all_bins = bins * owners
    assert (inner // 2) % bins == 0 and bins % LANES == 0 and half > 1

    def const(value, dtype):
        return jnp.asarray(value, dtype=dtype)

    ic, isn = angle_table(np.arange(inner), np.arange(inner // 2), inner)
    oc, osn = angle_table(np.arange(RADIX), np.arange(all_bins), sample_count)
    lag_ids = np.arange(NLAG) - NLAG // 2
    cc, cs = angle_table(np.arange(0, all_bins, STEP), lag_ids, sample_count)
    fc, fs = angle_table(np.arange(STEP), lag_ids, sample_count)
    vmem = pl.BlockSpec(memory_space=pltpu.VMEM)
    hbm = pl.BlockSpec(memory_space=pltpu.HBM)
    dma = pltpu.SemaphoreType.DMA
    peers = max(1, half - 1)
    operands = (
        traces, band_gain.reshape(1, bins), pair_list.T, pair_count.reshape(1, 1),
        const(np.stack([ic.reshape(inner, -1, LANES), -isn.reshape(inner, -1, LANES)], axis=2).reshape(inner, inner), jnp.bfloat16),
        const(np.concatenate([oc, -osn]), jnp.float32),
        const(np.stack([cc, cs]), jnp.float32),
        const(np.stack([fc, fs]), jnp.float32),
    )
    return pl.pallas_call(
        functools.partial(kernel, (chan_total, owners, reach)),
        out_shape=jax.ShapeDtypeStruct((group, NLAG), jnp.float32),
        in_specs=[hbm] * len(operands),
        out_specs=vmem,
        scratch_shapes=[
            *[pltpu.VMEM(x.shape, x.dtype) for x in operands],
            pltpu.VMEM(pair_list.shape, jnp.int32), dma((len(operands),)),
            pltpu.VMEM((bins // LANES, 2 * reach + 1, rows, 2 * LANES), jnp.bfloat16),
            pltpu.VMEM((2 * bins, NLAG), jnp.bfloat16),
            pltpu.VMEM((owners * group, NLAG), jnp.float32),
            pltpu.VMEM((half * group, NLAG), jnp.bfloat16),
            pltpu.VMEM((half * group, NLAG), jnp.bfloat16),
            pltpu.VMEM((peers * group, NLAG), jnp.bfloat16),
            pltpu.VMEM((peers * group, NLAG), jnp.bfloat16),
            dma((bins // LANES, 2 * reach)), dma((bins // LANES, 2 * reach)),
            dma((2,)), dma((2,)),
            dma((peers,)), dma((peers,)),
        ],
        compiler_params=pltpu.CompilerParams(
            collective_id=0, has_side_effects=True, vmem_limit_bytes=int(VMEM_MIB * 1024 * 1024)
        ),
        name="correlate",
    )(*operands)


def solution(mesh):
    placed = (P("chan", None), P("off"), P("chan", None), P(("chan", "off")))
    return jax.shard_map(
        shards, mesh=mesh, in_specs=placed, out_specs=P(("chan", "off"), None), check_vma=False
    )
```

```python
import functools
import math

import jax
import jax.numpy as jnp
import numpy as np
from jax import lax
from jax.experimental import pallas as pl
from jax.experimental.pallas import tpu as pltpu
from jax.sharding import PartitionSpec as P

NLAG = 1024
BAND = 64
RADIX = 4
LANES = 128
STEP = 64
VMEM_MIB = 58
MESH = pl.DeviceIdType.MESH


def angle_table(rows, cols, period):
    turns = np.mod(np.outer(rows, cols), period).astype(np.float64) * (2.0 * math.pi / period)
    return np.cos(turns), np.sin(turns)


def kernel(
    sizes,
    traces_hbm, gain_hbm, pairs_hbm, limit_hbm, inner_hbm, outer_hbm, coarse_hbm, fine_hbm,
    out_ref,
    traces_ref, gain_ref, pairs_ref, limit_ref, inner_ref, outer_ref, coarse_ref, fine_ref, slots, load_sem,
    table, inverse, total, swap_send, swap_recv, sum_send, sum_recv,
    chan_send_sem, chan_recv_sem, swap_send_sem, swap_recv_sem, off_send_sem, off_recv_sem,
):
    chan_total, owners, reach = sizes
    rows, sample_count = traces_ref.shape
    bins = gain_ref.shape[1]
    group = out_ref.shape[0]
    half = owners // 2
    pieces = bins // LANES
    me_chan = lax.axis_index("chan")
    me_off = lax.axis_index("off")
    bin_lo = me_off * bins
    parity = lax.rem(me_off, 2)
    my_half = lax.div(me_off, 2)
    partner = me_off + 1 - 2 * parity

    def chan_peer(shift):
        return lax.rem(me_chan + shift + chan_total, chan_total)

    def off_peer(step):
        return 2 * lax.rem(my_half + step, half) + parity

    loads = [
        pltpu.make_async_copy(source, target, load_sem.at[i])
        for i, (source, target) in enumerate(
            (
                (traces_hbm, traces_ref), (inner_hbm, inner_ref), (outer_hbm, outer_ref), (gain_hbm, gain_ref),
                (fine_hbm, fine_ref), (coarse_hbm, coarse_ref), (pairs_hbm, pairs_ref), (limit_hbm, limit_ref),
            )
        )
    ]
    for load in loads:
        load.start()

    shifts = [s for d in range(reach, 0, -1) for s in (d, -d)]
    relayed = pieces - 1 if reach == 2 and chan_total % 2 == 0 else 0
    side = 1 - 2 * lax.rem(me_chan, 2)
    barrier = pltpu.get_barrier_semaphore()
    for shift in shifts:
        pl.semaphore_signal(barrier, inc=1, device_id=(chan_peer(shift), me_off), device_id_type=MESH)
    pl.semaphore_signal(barrier, inc=1, device_id=(me_chan, partner), device_id_type=MESH)
    for step in range(1, half):
        pl.semaphore_signal(barrier, inc=1, device_id=(me_chan, off_peer(step)), device_id_type=MESH)

    inner = sample_count // RADIX
    chunk = RADIX * LANES
    chunks = sample_count // chunk
    odd_half = lax.rem(lax.div(bin_lo, inner // 2), 2)
    src = lax.broadcasted_iota(jnp.int32, (chunk, chunk), 0)
    dst = lax.broadcasted_iota(jnp.int32, (1, chunk), 1)
    lane = jnp.bitwise_and(dst, LANES - 1)
    wanted = RADIX * lane + jnp.right_shift(dst, LANES.bit_length() - 1)
    flip = 1.0 - 2.0 * (jnp.bitwise_and(lane, 1) * odd_half).astype(jnp.float32)
    spread = jnp.where(src == wanted, flip, 0.0).astype(jnp.bfloat16)
    band_a = jnp.right_shift(lax.broadcasted_iota(jnp.int32, (LANES, LANES), 0), BAND.bit_length() - 1)
    band_b = jnp.right_shift(lax.broadcasted_iota(jnp.int32, (LANES, LANES), 1), BAND.bit_length() - 1)
    mean_of = jnp.where(band_a == band_b, 1.0 / BAND, 0.0).astype(jnp.bfloat16)
    loads[0].wait()
    stacked = jnp.concatenate([traces_ref[:, c * chunk:(c + 1) * chunk] for c in range(chunks)], axis=0)
    split = jnp.dot(stacked, spread, preferred_element_type=jnp.float32).astype(jnp.bfloat16)
    by_residue = jnp.concatenate(
        [
            jnp.concatenate(
                [split[c * rows:(c + 1) * rows, r * LANES:(r + 1) * LANES] for c in range(chunks)], axis=1
            )
            for r in range(RADIX)
        ],
        axis=0,
    )
    for load in loads[1:4]:
        load.wait()
    col_lo = lax.rem(bin_lo, inner // 2)

    def send_block(q, i, source, target, shift):
        move = pltpu.make_async_remote_copy(
            src_ref=table.at[q, source],
            dst_ref=table.at[q, target],
            send_sem=chan_send_sem.at[q, i],
            recv_sem=chan_recv_sem.at[q, i],
            device_id=(chan_peer(shift), me_off),
            device_id_type=MESH,
        )
        move.start()
        return move

    moves = []
    for q in range(pieces):
        at = pl.multiple_of(2 * (col_lo + q * LANES), LANES)
        part = jnp.dot(by_residue, inner_ref[:, pl.ds(at, 2 * LANES)], preferred_element_type=jnp.float32)
        real_part = part[:rows, :LANES]
        imag_part = part[:rows, LANES:]
        tw = pl.ds(pl.multiple_of(bin_lo + q * LANES, LANES), LANES)
        for r in range(1, RADIX):
            tc = outer_ref[r:r + 1, tw]
            ts = outer_ref[RADIX + r:RADIX + r + 1, tw]
            a = part[r * rows:(r + 1) * rows, :LANES]
            b = part[r * rows:(r + 1) * rows, LANES:]
            real_part += a * tc - b * ts
            imag_part += a * ts + b * tc
        power = real_part * real_part + imag_part * imag_part
        high = power.astype(jnp.bfloat16)
        low = (power - high.astype(jnp.float32)).astype(jnp.bfloat16)
        mean = jnp.dot(high, mean_of, preferred_element_type=jnp.float32) + jnp.dot(
            low, mean_of, preferred_element_type=jnp.float32
        )
        scale = lax.rsqrt(mean + 1e-06) * gain_ref[:, q * LANES:(q + 1) * LANES]
        table[q, reach, :, :LANES] = (real_part * scale).astype(jnp.bfloat16)
        table[q, reach, :, LANES:] = (imag_part * scale).astype(jnp.bfloat16)
        if q == 0:
            pl.semaphore_wait(barrier, len(shifts) + half)
        moves.append([])
        for i, shift in enumerate(shifts):
            near = q < relayed and abs(shift) == 1
            if near and shift == -1:
                continue
            if near:
                shift = side
            moves[q].append(send_block(q, i, reach, reach - shift, shift))

    for load in loads[4:]:
        load.wait()
    slots[...] = jnp.transpose(pairs_ref[...])
    row_lo = lax.div(bin_lo, STEP)
    per = LANES // STEP

    def fill(a, carry):
        cc = coarse_ref[0, pl.ds(row_lo + a, 1), :]
        cs = coarse_ref[1, pl.ds(row_lo + a, 1), :]
        fc = fine_ref[0]
        fs = fine_ref[1]
        at = pl.multiple_of(a // per * 2 * LANES + a % per * STEP, STEP)
        inverse[pl.ds(at, STEP), :] = (cc * fc - cs * fs).astype(jnp.bfloat16)
        inverse[pl.ds(LANES + at, STEP), :] = (-(cs * fc + cc * fs)).astype(jnp.bfloat16)
        return carry

    lax.fori_loop(0, bins // STEP, fill, 0)

    span = (2 * reach + 1) * rows
    chan_a = me_chan * rows + lax.broadcasted_iota(jnp.int32, (1, rows), 1)
    chan_b = (me_chan - reach) * rows + lax.broadcasted_iota(jnp.int32, (1, span), 1)
    chan_b = jnp.where(chan_b < 0, chan_b + chan_total * rows, chan_b)
    chan_b = jnp.where(chan_b >= chan_total * rows, chan_b - chan_total * rows, chan_b)
    far = (half - 1) * group
    order = [off_peer(s) + 1 - 2 * parity for s in range(1, half)] + [off_peer(s) for s in range(1, half)]
    order += [partner, me_off]
    pairs = jnp.concatenate(
        [slots[pl.ds(pl.multiple_of(o * group, group), group), :] for o in order], axis=0
    )
    pick_a = jnp.where(pairs[:, 0:1] == chan_a, 1.0, 0.0).astype(jnp.bfloat16)
    pick_b = jnp.where(pairs[:, 1:2] == chan_b, 1.0, 0.0).astype(jnp.bfloat16)

    def product(q, lo, hi):
        left = jnp.dot(pick_a[lo:hi], table[q, reach], preferred_element_type=jnp.float32)
        right = jnp.dot(
            pick_b[lo:hi], table[q].reshape(span, 2 * LANES), preferred_element_type=jnp.float32
        )
        la, lb = left[:, :LANES], left[:, LANES:]
        ra, rb = right[:, :LANES], right[:, LANES:]
        cross = jnp.concatenate([la * ra + lb * rb, la * rb - lb * ra], axis=1).astype(jnp.bfloat16)
        return jnp.dot(
            cross, inverse[q * 2 * LANES:(q + 1) * 2 * LANES, :], preferred_element_type=jnp.float32
        )

    def swap(index, lo, count):
        copy = pltpu.make_async_remote_copy(
            src_ref=swap_send.at[pl.ds(lo, count), :],
            dst_ref=swap_recv.at[pl.ds(lo, count), :],
            send_sem=swap_send_sem.at[index],
            recv_sem=swap_recv_sem.at[index],
            device_id=(me_chan, partner),
            device_id_type=MESH,
        )
        copy.start()
        return copy

    everything = 2 * far + 2 * group
    for q in range(relayed):
        for move in moves[q][:2]:
            move.wait_recv()
        moves[q].append(send_block(q, len(shifts) - 1, reach + 2 * side, reach + side, side))
    for q in range(pieces - 1):
        for move in moves[q][2 if q < relayed else 0:]:
            move.wait_recv()
        if q == 0:
            total[...] = product(q, 0, everything)
        else:
            total[...] += product(q, 0, everything)
    for move in moves[pieces - 1]:
        move.wait_recv()

    def last(lo, hi):
        value = product(pieces - 1, lo, hi)
        return value + total[lo:hi, :] if pieces > 1 else value

    outer_rows = last(0, 2 * far)
    swap_send[:far, :] = outer_rows[:far].astype(swap_send.dtype)
    swap_far = swap(0, 0, far)
    total[far:2 * far, :] = outer_rows[far:]
    near_rows = last(2 * far, everything)
    swap_send[far:, :] = near_rows[:group].astype(swap_send.dtype)
    swap_near = swap(1, far, group)
    out_ref[...] = near_rows[group:]
    swap_far.wait_recv()
    sends = []
    for step in range(1, half):
        lo = (step - 1) * group
        sum_send[lo:lo + group, :] = (
            total[far + lo:far + lo + group, :] + swap_recv[lo:lo + group, :].astype(jnp.float32)
        ).astype(sum_send.dtype)
        send = pltpu.make_async_remote_copy(
            src_ref=sum_send.at[pl.ds(lo, group), :],
            dst_ref=sum_recv.at[pl.ds(lo, group), :],
            send_sem=off_send_sem.at[step - 1],
            recv_sem=off_recv_sem.at[step - 1],
            device_id=(me_chan, off_peer(step)),
            device_id_type=MESH,
        )
        send.start()
        sends.append(send)
    swap_near.wait_recv()
    result = out_ref[...] + swap_recv[far:, :].astype(jnp.float32)
    for step in range(1, half):
        sends[step - 1].wait_recv()
        result += sum_recv[(step - 1) * group:step * group, :].astype(jnp.float32)
    live = lax.broadcasted_iota(jnp.int32, (group, 1), 0) < limit_ref[...]
    out_ref[...] = jnp.where(live, result * (1.0 / math.sqrt(sample_count // 2)), 0.0)
    for copy in [move for piece in moves for move in piece] + [swap_far, swap_near] + sends:
        copy.wait_send()


def shards(traces, band_gain, pair_list, pair_count):
    chan_total = lax.axis_size("chan")
    owners = lax.axis_size("off")
    reach = chan_total // 4
    rows, sample_count = traces.shape
    bins = band_gain.shape[0]
    group = pair_list.shape[0] // owners
    half = owners // 2
    inner = sample_count // RADIX
    all_bins = bins * owners
    assert (inner // 2) % bins == 0 and bins % LANES == 0 and half > 1

    def const(value, dtype):
        return jnp.asarray(value, dtype=dtype)

    ic, isn = angle_table(np.arange(inner), np.arange(inner // 2), inner)
    oc, osn = angle_table(np.arange(RADIX), np.arange(all_bins), sample_count)
    lag_ids = np.arange(NLAG) - NLAG // 2
    cc, cs = angle_table(np.arange(0, all_bins, STEP), lag_ids, sample_count)
    fc, fs = angle_table(np.arange(STEP), lag_ids, sample_count)
    vmem = pl.BlockSpec(memory_space=pltpu.VMEM)
    hbm = pl.BlockSpec(memory_space=pltpu.HBM)
    dma = pltpu.SemaphoreType.DMA
    peers = max(1, half - 1)
    operands = (
        traces, band_gain.reshape(1, bins), pair_list.T, pair_count.reshape(1, 1),
        const(np.stack([ic.reshape(inner, -1, LANES), -isn.reshape(inner, -1, LANES)], axis=2).reshape(inner, inner), jnp.bfloat16),
        const(np.concatenate([oc, -osn]), jnp.float32),
        const(np.stack([cc, cs]), jnp.float32),
        const(np.stack([fc, fs]), jnp.float32),
    )
    return pl.pallas_call(
        functools.partial(kernel, (chan_total, owners, reach)),
        out_shape=pltpu.VMEM((group, NLAG), jnp.float32),
        in_specs=[hbm] * len(operands),
        out_specs=vmem,
        scratch_shapes=[
            *[pltpu.VMEM(x.shape, x.dtype) for x in operands],
            pltpu.VMEM(pair_list.shape, jnp.int32), dma((len(operands),)),
            pltpu.VMEM((bins // LANES, 2 * reach + 1, rows, 2 * LANES), jnp.bfloat16),
            pltpu.VMEM((2 * bins, NLAG), jnp.bfloat16),
            pltpu.VMEM((owners * group, NLAG), jnp.float32),
            pltpu.VMEM((half * group, NLAG), jnp.bfloat16),
            pltpu.VMEM((half * group, NLAG), jnp.bfloat16),
            pltpu.VMEM((peers * group, NLAG), jnp.bfloat16),
            pltpu.VMEM((peers * group, NLAG), jnp.bfloat16),
            dma((bins // LANES, 2 * reach)), dma((bins // LANES, 2 * reach)),
            dma((2,)), dma((2,)),
            dma((peers,)), dma((peers,)),
        ],
        compiler_params=pltpu.CompilerParams(
            collective_id=0, has_side_effects=True, vmem_limit_bytes=int(VMEM_MIB * 1024 * 1024)
        ),
        name="correlate",
    )(*operands)


def solution(mesh):
    placed = (P("chan", None), P("off"), P("chan", None), P(("chan", "off")))
    return jax.shard_map(
        shards, mesh=mesh, in_specs=placed, out_specs=P(("chan", "off"), None), check_vma=False
    )
```
